128 devices in a mesh: ctx: 16 (over y, x), ch: 8 (over z, core).
Axes of the slice: x: 4, y: 4, z: 4, core: 2. Of those that a mesh axis runs over, the one named last changes fastest.
Arguments:
- projected: bfloat16 [2048, 3, 8192], P('ctx', None, 'ch'), may hold values from -6 to 6
- short_filter: float32 [3, 3, 8192], P(None, None, 'ch'), may hold values from -2.5 to 2.5
- decay_rate: float32 [16, 8192], P(None, 'ch'), as said below
- residue: float32 [16, 8192], P(None, 'ch'), as said below
- skip: float32 [8192], P('ch'), may hold values from -4 to 4
- state_in: float32 [16, 8192], P(None, 'ch'), as said below
- out_weight: bfloat16 [8192, 8192], P('ch'), may hold values from -0.09375 to 0.09375
- cotangent: bfloat16 [2048, 8192], P('ctx', 'ch'), may hold values from -6 to 6
Outputs:
- mixed_out: bfloat16 [2048, 8192], P('ctx', 'ch')
- grad_projected: bfloat16 [2048, 3, 8192], P('ctx', None, 'ch')
- grad_weight: bfloat16 [8192, 8192], P('ctx', 'ch')
- grad_filter: float32 [3, 3, 8192], P(None, None, 'ch')
- grad_residue: float32 [16, 8192], P(None, 'ch')
- grad_skip: float32 [8192], P('ch')
- grad_state: float32 [16, 8192], P(None, 'ch')
The draws below stay inside these ranges and needn't reach their ends.
Inputs may be any that keep to these rules, and one draw needn't show every extreme that they name: `decay_rate`: every rate lies between 0.1 / 2048 and 0.05. `residue`: residues are real numbers of either sign. `state_in`: state entries are real numbers of either sign.
All inputs are finite; a program needn't handle non-finite values.
Results may differ from the reference program's by a relative error of at most 0.019.
Values may be sent and summed in bfloat16 or wider, within the bound.
No kernel may reach another device: no remote copies, remote signals or barrier semaphores. Data moves between devices by JAX's collectives and lax.ppermute only.
A program may use at most 192 MiB of HBM per device.

```python
import jax
import jax.numpy as jnp
from jax import lax

D = 8192
MODES = 16
KSHORT = 3
TOK_DEV = 128
TOKENS = 2048
N_CTX = 16
N_CH = 8


def mode_rates(key):
    folded = jax.random.fold_in(key, 4101)
    pick_key, slow_key, fast_key = jax.random.split(folded, 3)
    shape_pair = (MODES, D)
    slow_rates = jnp.exp(jax.random.uniform(slow_key, shape_pair, jnp.float32, jnp.log(0.1 / TOKENS), jnp.log(2.0 / TOKENS)))
    fast_rates = jnp.exp(jax.random.uniform(fast_key, shape_pair, jnp.float32, jnp.log(2.0 / TOKENS), jnp.log(0.05)))
    slow_share = 0.5
    chooser = jax.random.uniform(pick_key, shape_pair, jnp.float32)
    return jnp.where(chooser < slow_share, slow_rates, fast_rates)


def draw_decay_rate(key, part):
    return mode_rates(key)


def draw_residue(key, part):
    rates = mode_rates(key)
    noise_key = jax.random.fold_in(key, 4102)
    noise = jax.random.normal(noise_key, (MODES, D), jnp.float32)
    return noise * jnp.sqrt(2.0 * rates) * 0.5


def draw_state_in(key, part):
    rates = mode_rates(key)
    noise_key = jax.random.fold_in(key, 4103)
    noise = jax.random.normal(noise_key, (MODES, D), jnp.float32)
    return noise * jnp.sqrt(jnp.minimum(0.5 / rates, 1.0 * TOKENS))


def raised(array, stream_key, source, target, parts, factor):
    owner, partner = [(jnp.arange(array.shape[dim]) // (array.shape[dim] // parts)).reshape([-1 if axis == dim else 1 for axis in range(array.ndim)]) for dim in (source, target)]
    chosen = jax.random.permutation(stream_key, parts)[partner]
    strong = (owner == chosen) | (owner == (partner + parts // 2) % parts)
    return jnp.where(strong, factor * array, array)


def block_levels(stream_key, shape, cuts, least, largest):
    factor_of, own = 1.0, jax.random.fold_in(stream_key, 6)
    for axis_at, parts in cuts:
        heights = jnp.exp(jax.random.uniform(jax.random.fold_in(own, axis_at), (parts,), jnp.float32, least / len(cuts), largest / len(cuts)))
        factor_of = factor_of * jnp.repeat(heights, shape[axis_at] // parts).reshape([-1 if axis == axis_at else 1 for axis in range(len(shape))])
    return factor_of


def gaussian(key, extent, scale, most, cuts=(), held_as=jnp.bfloat16):
    factor_of = block_levels(key, extent, cuts, -0.22, 0.18) if cuts else 1.0
    array = jax.random.normal(key, extent, jnp.float32) * scale * factor_of
    return jnp.minimum(jnp.maximum(array, -most), most).astype(held_as)


def bell_draw_with(stream_key, dims, scale, limit, cuts, heavy, held_as=jnp.bfloat16):
    entries = scale * jax.random.normal(stream_key, dims, jnp.float32)
    if cuts:
        entries = entries * block_levels(stream_key, dims, cuts, -0.22, 0.18)
    return jnp.clip(raised(entries, jax.random.fold_in(stream_key, 3), *heavy), -limit, limit).astype(held_as)


def setup_inputs(seed: int = 0) -> dict:
    key_list = jax.random.split(jax.random.key(seed), 9)
    projected = gaussian(key_list[0], (TOKENS, 3, D), 1.0, 6.0, ((0, 16), (2, 8)))
    short_filter = gaussian(key_list[1], (3, KSHORT, D), 0.4, 2.5, ((2, 8),), jnp.float32)
    decay_rate = draw_decay_rate(jax.random.fold_in(key_list[8], 71), 0)
    residue = draw_residue(jax.random.fold_in(key_list[8], 71), 0)
    skip = gaussian(key_list[4], (D,), 1.0, 4.0, ((0, 8),), jnp.float32)
    state_in = draw_state_in(jax.random.fold_in(key_list[8], 71), 0)
    out_weight = bell_draw_with(key_list[6], (D, D), D ** -0.5, 0.09375, ((0, 8),), (0, 1, 8, 2.0))
    cotangent = bell_draw_with(key_list[7], (TOKENS, D), 1.0, 6.0, ((0, 16), (1, 8)), (0, 1, 16, 2.0))
    return dict(projected=projected, short_filter=short_filter, decay_rate=decay_rate, residue=residue, skip=skip, state_in=state_in, out_weight=out_weight, cotangent=cotangent)


def featurize(streams, filters):
    total_rows = streams.shape[0]
    taps = filters.shape[1]
    rim_rows = taps - 1
    padded = jnp.concatenate([jnp.zeros((rim_rows,) + streams.shape[1:], jnp.float32), streams.astype(jnp.float32)], 0)
    featurized = padded[rim_rows:] * filters[None, :, 0, :]
    for offset in range(1, taps):
        featurized = featurized + padded[rim_rows - offset: rim_rows - offset + total_rows] * filters[None, :, offset, :]
    return featurized, padded


def reference(projected, short_filter, decay_rate, residue, skip, state_in, out_weight, cotangent):
    total_rows = projected.shape[0]
    width_all = projected.shape[2]
    chan_block = width_all // N_CH
    taps = short_filter.shape[1]
    rim_rows = taps - 1
    block_ids = jnp.arange(N_CH, dtype=jnp.int32)

    def pieces(block_id):
        begin = (block_id * chan_block).astype(jnp.int32)
        streams = lax.dynamic_slice_in_dim(projected, begin, chan_block, 2)
        filters = lax.dynamic_slice_in_dim(short_filter, begin, chan_block, 2)
        rates = lax.dynamic_slice_in_dim(decay_rate, begin, chan_block, 1)
        weights = lax.dynamic_slice_in_dim(residue, begin, chan_block, 1)
        direct = lax.dynamic_slice_in_dim(skip, begin, chan_block, 0)
        initial = lax.dynamic_slice_in_dim(state_in, begin, chan_block, 1)
        return begin, streams, filters, rates, weights, direct, initial

    def forward_block(block_id):
        begin, streams, filters, rates, weights, direct, initial = pieces(block_id)
        featurized, padded = featurize(streams, filters)
        product = featurized[:, 1] * featurized[:, 2]
        pole = jnp.exp(-rates)

        def advance(carry, item):
            carry = pole * carry + item[None]
            return carry, jnp.sum(weights * carry, 0)

        final_state, long_mix = lax.scan(advance, initial, product)
        combined = long_mix + direct[None] * product
        return (featurized[:, 0] * combined).astype(jnp.bfloat16)

    gated_blocks = lax.map(forward_block, block_ids)
    gated = jnp.moveaxis(gated_blocks, 0, 1).reshape(total_rows, width_all)

    def add_partial(block_id, total):
        begin = (block_id * chan_block).astype(jnp.int32)
        gated_part = lax.dynamic_slice_in_dim(gated, begin, chan_block, 1)
        weight_part = lax.dynamic_slice_in_dim(out_weight, begin, chan_block, 0)
        partial_sum = jnp.dot(gated_part, weight_part, preferred_element_type=jnp.float32)
        return total + lax.optimization_barrier(partial_sum.astype(jnp.bfloat16)).astype(jnp.float32)

    mixed_out = lax.fori_loop(0, N_CH, add_partial, jnp.zeros((total_rows, width_all), jnp.float32)).astype(jnp.bfloat16)

    def add_tokens(token_block, total):
        begin = (token_block * TOK_DEV).astype(jnp.int32)
        grad_part = lax.dynamic_slice_in_dim(cotangent, begin, TOK_DEV, 0)
        gated_part = lax.dynamic_slice_in_dim(gated, begin, TOK_DEV, 0)
        partial_sum = lax.dot_general(grad_part, gated_part, (((0,), (0,)), ((), ())), preferred_element_type=jnp.float32)
        return total + lax.optimization_barrier(partial_sum.astype(jnp.bfloat16)).astype(jnp.float32)

    grad_weight = lax.fori_loop(0, N_CTX, add_tokens, jnp.zeros((width_all, width_all), jnp.float32)).astype(jnp.bfloat16)

    grad_gated = lax.dot_general(cotangent, out_weight, (((1,), (1,)), ((), ())), preferred_element_type=jnp.float32)

    def backward_block(block_id):
        begin, streams, filters, rates, weights, direct, initial = pieces(block_id)
        featurized, padded = featurize(streams, filters)
        product = featurized[:, 1] * featurized[:, 2]
        pole = jnp.exp(-rates)
        grad_here = lax.dynamic_slice_in_dim(grad_gated, begin, chan_block, 1)
        grad_combined = grad_here * featurized[:, 0]

        def advance(carry, item):
            state_now, accumulated = carry
            source, grad_now = item
            state_now = pole * state_now + source[None]
            return (state_now, accumulated + state_now * grad_now[None]), jnp.sum(weights * state_now, 0)

        (final_state, grad_residue), long_mix = lax.scan(advance, (initial, jnp.zeros_like(initial)), (product, grad_combined))
        combined = long_mix + direct[None] * product

        def retreat(carry, grad_now):
            carry = pole * carry + grad_now[None]
            return carry, jnp.sum(weights * carry, 0)

        adjoint_first, adjoint_mix = lax.scan(retreat, jnp.zeros_like(initial), grad_combined, reverse=True)
        grad_product = direct[None] * grad_combined + adjoint_mix
        grad_skip = jnp.sum(grad_combined * product, 0)
        grad_state = weights * pole * adjoint_first
        grad_featurized = jnp.stack([grad_here * combined, grad_product * featurized[:, 2], grad_product * featurized[:, 1]], 1)
        extended = jnp.concatenate([grad_featurized, jnp.zeros((rim_rows,) + grad_featurized.shape[1:], jnp.float32)], 0)
        grad_streams = extended[:total_rows] * filters[None, :, 0, :]
        for offset in range(1, taps):
            grad_streams = grad_streams + extended[offset: offset + total_rows] * filters[None, :, offset, :]
        grad_filters = jnp.stack([jnp.sum(grad_featurized * padded[rim_rows - offset: rim_rows - offset + total_rows], 0) for offset in range(taps)], 1)
        return grad_streams.astype(jnp.bfloat16), grad_filters, grad_residue, grad_skip, grad_state

    grad_streams, grad_filters, grad_residues, grad_skips, grad_states = lax.map(backward_block, block_ids)
    grad_projected = jnp.moveaxis(grad_streams, 0, 2).reshape(total_rows, 3, width_all)
    grad_filter = jnp.moveaxis(grad_filters, 0, 2).reshape(3, taps, width_all)
    grad_residue = jnp.moveaxis(grad_residues, 0, 1).reshape(grad_residues.shape[1], width_all)
    grad_skip = grad_skips.reshape(width_all)
    grad_state = jnp.moveaxis(grad_states, 0, 1).reshape(grad_states.shape[1], width_all)
    return mixed_out, grad_projected, grad_weight, grad_filter, grad_residue, grad_skip, grad_state
```

```python
import jax
import jax.numpy as jnp
from jax import lax
from jax.experimental import pallas as pl
from jax.experimental.pallas import tpu as pltpu
from jax.sharding import PartitionSpec as P

F32 = jnp.float32
BF16 = jnp.bfloat16
TOK = 128
CH = 1024
MODES = 16
TAPS = 3
NCTX = 16
NCH = 8
ROWS = TOK * 8
SMALL = 9 + MODES + 1

VMEM = pl.BlockSpec(memory_space=pltpu.VMEM)
SMEM = pl.BlockSpec(memory_space=pltpu.SMEM)


def cost(flops, moved):
    return pl.CostEstimate(flops=flops, bytes_accessed=moved, transcendentals=0)


def fold(dst, base, src, count):
    for k in range(8):
        dst[pl.ds(base * 8 + k, count, stride=8), :] = src(slice(k * 128, (k + 1) * 128))


def tile(ref, row):
    return ref[pl.ds(pl.multiple_of(row * 8, 8), 8), :]


def fold_small(dst, src_ref, count):
    for r in range(count):
        for k in range(8):
            dst[r * 8 + k : r * 8 + k + 1, :] = src_ref[r : r + 1, k * 128 : (k + 1) * 128]


def fold_filter(dst, filt_ref):
    for j in range(3):
        for s in range(TAPS):
            for k in range(8):
                r = (j * 3 + s) * 8 + k
                dst[r : r + 1, :] = filt_ref[j, s : s + 1, k * 128 : (k + 1) * 128]


def kernel_a(proj, halo, filt, rate, feat, rows, totals, wf, rt):
    fold_filter(wf, filt)
    fold(rt, 0, lambda c: rate[:, c], MODES)
    for j in range(3):
        for r in range(2):
            for k in range(8):
                rows[j, r * 8 + k : r * 8 + k + 1, :] = halo[
                    j, r : r + 1, k * 128 : (k + 1) * 128
                ].astype(F32)
        for k in range(8):
            rows[j, pl.ds(16 + k, TOK, stride=8), :] = proj[
                j, :, k * 128 : (k + 1) * 128
            ].astype(F32)
    poles = [jnp.exp(-tile(rt, m)) for m in range(MODES)]
    taps = [[tile(wf, j * 3 + s) for s in range(TAPS)] for j in range(3)]

    def token(t, states):
        out = []
        for j in range(3):
            value = taps[j][0] * tile(rows.at[j], t + 2)
            value = value + taps[j][1] * tile(rows.at[j], t + 1)
            value = value + taps[j][2] * tile(rows.at[j], t)
            feat[j, pl.ds(pl.multiple_of(t * 8, 8), 8), :] = value
            out.append(value)
        product = out[1] * out[2]
        return tuple(poles[m] * states[m] + product for m in range(MODES))

    zero = jnp.zeros((8, 128), F32)
    states = lax.fori_loop(0, TOK, token, (zero,) * MODES, unroll=4)
    for m in range(MODES):
        totals[m * 8 : m * 8 + 8, :] = states[m].astype(BF16)


def call_a(proj, halo, filt, rate):
    return pl.pallas_call(
        kernel_a,
        out_shape=(
            jax.ShapeDtypeStruct((3, ROWS, 128), F32),
            jax.ShapeDtypeStruct((3, ROWS + 16, 128), F32),
            jax.ShapeDtypeStruct((MODES * 8, 128), BF16),
        ),
        in_specs=[VMEM] * 4,
        out_specs=(VMEM,) * 3,
        scratch_shapes=[pltpu.VMEM((72, 128), F32), pltpu.VMEM((MODES * 8, 128), F32)],
        cost_estimate=cost(10_000_000, 6_000_000),
        name="feat",
    )(proj, halo, filt, rate)


def kernel_b(pos, gathered, state_in, rate, res, skip, feat, gated, comb, incoming, rt, rs, g):
    fold(rt, 0, lambda c: rate[:, c], MODES)
    fold(rs, 0, lambda c: res[:, c], MODES)
    fold(incoming, 0, lambda c: state_in[:, c], MODES)
    me = pos[0]
    for m in range(MODES):
        across = jnp.exp(tile(rt, m) * (-float(TOK)))

        def relay(i, state, across=across, m=m):
            total = gathered[i, m * 8 : m * 8 + 8, :].astype(F32)
            return across * state + total

        incoming[m * 8 : m * 8 + 8, :] = lax.fori_loop(0, me, relay, tile(incoming, m))
    poles = [jnp.exp(-tile(rt, m)) for m in range(MODES)]
    weights = [tile(rs, m) for m in range(MODES)]
    direct = jnp.concatenate([skip[:, k * 128 : (k + 1) * 128] for k in range(8)], 0)

    def token(t, states):
        product = tile(feat.at[1], t) * tile(feat.at[2], t)
        total = direct * product
        new = []
        parts = [None, None, None, None]
        for m in range(MODES):
            state = poles[m] * states[m] + product
            term = weights[m] * state
            parts[m % 4] = term if parts[m % 4] is None else parts[m % 4] + term
            new.append(state)
        total = total + ((parts[0] + parts[1]) + (parts[2] + parts[3]))
        at = pl.ds(pl.multiple_of(t * 8, 8), 8)
        comb[at, :] = total
        g[at, :] = tile(feat.at[0], t) * total
        return tuple(new)

    lax.fori_loop(0, TOK, token, tuple(tile(incoming, m) for m in range(MODES)), unroll=2)
    for k in range(8):
        gated[:, k * 128 : (k + 1) * 128] = g[pl.ds(k, TOK, stride=8), :].astype(BF16)


def call_b(pos, gathered, state_in, rate, res, skip, feat):
    return pl.pallas_call(
        kernel_b,
        out_shape=(
            jax.ShapeDtypeStruct((TOK, CH), BF16),
            jax.ShapeDtypeStruct((ROWS, 128), F32),
            jax.ShapeDtypeStruct((MODES * 8, 128), F32),
        ),
        in_specs=[SMEM] + [VMEM] * 6,
        out_specs=(VMEM,) * 3,
        scratch_shapes=[
            pltpu.VMEM((MODES * 8, 128), F32),
            pltpu.VMEM((MODES * 8, 128), F32),
            pltpu.VMEM((ROWS, 128), F32),
        ],
        cost_estimate=cost(10_000_000, 6_000_000),
        name="gate",
    )(pos, gathered, state_in, rate, res, skip, feat)


def kernel_c(gg, rate, feat, comb, rows, ggr, first, rim, rt):
    fold(rt, 0, lambda c: rate[:, c], MODES)
    fold(ggr, 0, lambda c: gg[:, c], TOK)
    poles = [jnp.exp(-tile(rt, m)) for m in range(MODES)]

    def token(i, adj):
        t = TOK - 1 - i
        here = tile(ggr, t) * tile(feat.at[0], t)
        return tuple(poles[m] * adj[m] + here for m in range(MODES))

    zero = jnp.zeros((8, 128), F32)
    adj = lax.fori_loop(0, TOK, token, (zero,) * MODES, unroll=4)
    for m in range(MODES):
        first[m * 8 : m * 8 + 8, :] = adj[m].astype(BF16)
    rim[0:16, :] = ggr[0:16, :].astype(BF16)
    rim[16:32, :] = comb[0:16, :].astype(BF16)
    for j in range(3):
        rim[32 + 16 * j : 48 + 16 * j, :] = rows[j, 16:32, :].astype(BF16)


def call_c(gg, rate, feat, comb, rows):
    return pl.pallas_call(
        kernel_c,
        out_shape=(
            jax.ShapeDtypeStruct((ROWS, 128), F32),
            jax.ShapeDtypeStruct((MODES * 8, 128), BF16),
            jax.ShapeDtypeStruct((80, 128), BF16),
        ),
        in_specs=[VMEM] * 5,
        out_specs=(VMEM,) * 3,
        scratch_shapes=[pltpu.VMEM((MODES * 8, 128), F32)],
        cost_estimate=cost(10_000_000, 6_000_000),
        name="adjoint_total",
    )(gg, rate, feat, comb, rows)


def kernel_d(
    pos, firsts, rim, rate, res, skip, filt, feat, rows, ggr, comb, incoming,
    gproj, small, gstate, rt, rs, wf, gp, acc, low,
):
    fold(rt, 0, lambda c: rate[:, c], MODES)
    fold(rs, 0, lambda c: res[:, c], MODES)
    fold_filter(wf, filt)
    me = pos[0]
    zero = jnp.zeros((8, 128), F32)
    poles = [jnp.exp(-tile(rt, m)) for m in range(MODES)]
    weights = [tile(rs, m) for m in range(MODES)]
    direct = jnp.concatenate([skip[:, k * 128 : (k + 1) * 128] for k in range(8)], 0)
    beyond = []
    for m in range(MODES):
        across = jnp.exp(tile(rt, m) * (-float(TOK)))

        def relay(i, state, across=across, m=m):
            total = firsts[NCTX - 1 - i, m * 8 : m * 8 + 8, :].astype(F32)
            return across * state + total

        after = lax.fori_loop(0, NCTX - 1 - me, relay, zero)
        whole = lax.fori_loop(NCTX - 1 - me, NCTX, relay, after)
        beyond.append(after)
        state_grad = weights[m] * poles[m] * whole
        for k in range(8):
            gstate[m : m + 1, k * 128 : (k + 1) * 128] = state_grad[k : k + 1, :]

    def rim_tile(r):
        return rim[r * 8 : r * 8 + 8, :].astype(F32)

    def taps(j, s):
        return tile(wf, j * 3 + s)

    gf_next = []
    adj = list(beyond)
    for r in range(2):
        f = []
        for j in range(3):
            p0 = rim_tile(4 + 2 * j + r)
            p1 = tile(rows.at[j], TOK + 1) if r == 0 else rim_tile(4 + 2 * j)
            p2 = tile(rows.at[j], TOK + r)
            f.append(taps(j, 0) * p0 + taps(j, 1) * p1 + taps(j, 2) * p2)
        here = rim_tile(r) * f[0]
        mix = direct * here
        for m in range(MODES):
            mix = mix + weights[m] * adj[m]
        gf_next.append((rim_tile(r) * rim_tile(2 + r), mix * f[2], mix * f[1]))
        if r == 0:
            adj = [(adj[m] - here) * jnp.exp(tile(rt, m)) for m in range(MODES)]

    def scan(i, states):
        t = TOK - 1 - i
        here = tile(ggr, t) * tile(feat.at[0], t)
        new = []
        parts = [direct * here, None, None, None]
        for m in range(MODES):
            state = poles[m] * states[m] + here
            term = weights[m] * state
            parts[m % 4] = term if parts[m % 4] is None else parts[m % 4] + term
            new.append(state)
        gp[pl.ds(pl.multiple_of(t * 8, 8), 8), :] = (parts[0] + parts[1]) + (parts[2] + parts[3])
        return tuple(new)

    lax.fori_loop(0, TOK, scan, tuple(beyond), unroll=2)

    for j in range(3):
        w = [taps(j, s) for s in range(TAPS)]

        def conv(i, carry, j=j, w=w):
            one, two, sums = carry
            t = TOK - 1 - i
            if j == 0:
                value = tile(ggr, t) * tile(comb, t)
            else:
                value = tile(gp, t) * tile(feat.at[3 - j], t)
            at = pl.ds(pl.multiple_of(t * 8, 8), 8)
            acc[j, at, :] = w[0] * value + w[1] * one + w[2] * two
            sums = tuple(sums[s] + value * tile(rows.at[j], t + 2 - s) for s in range(TAPS))
            return value, one, sums

        _, _, sums = lax.fori_loop(
            0, TOK, conv, (gf_next[0][j], gf_next[1][j], (zero,) * TAPS), unroll=4
        )
        for s in range(TAPS):
            r = (j * 3 + s) * 8
            small[r : r + 8, :] = sums[s].astype(BF16)
        for k in range(8):
            gproj[j, :, k * 128 : (k + 1) * 128] = acc[j, pl.ds(k, TOK, stride=8), :].astype(BF16)

    for half in range(2):
        modes = range(half * 8, half * 8 + 8)

        def again(t, carry, modes=modes, half=half):
            states, sums, total = carry
            product = tile(feat.at[1], t) * tile(feat.at[2], t)
            here = tile(ggr, t) * tile(feat.at[0], t)
            states = tuple(poles[m] * s + product for m, s in zip(modes, states))
            sums = tuple(a + here * s for a, s in zip(sums, states))
            if half == 0:
                total = total + here * product
            return states, sums, total

        start = tuple(tile(incoming, m) for m in modes)
        _, sums, total = lax.fori_loop(0, TOK, again, (start, (zero,) * 8, zero), unroll=2)
        for m, value in zip(modes, sums):
            small[(9 + m) * 8 : (10 + m) * 8, :] = value.astype(BF16)
        if half == 0:
            small[(9 + MODES) * 8 : (10 + MODES) * 8, :] = total.astype(BF16)


def call_d(pos, firsts, rim, rate, res, skip, filt, feat, rows, ggr, comb, incoming):
    return pl.pallas_call(
        kernel_d,
        out_shape=(
            jax.ShapeDtypeStruct((3, TOK, CH), BF16),
            jax.ShapeDtypeStruct((SMALL * 8, 128), BF16),
            jax.ShapeDtypeStruct((MODES, CH), F32),
        ),
        in_specs=[SMEM] + [VMEM] * 11,
        out_specs=(VMEM,) * 3,
        scratch_shapes=[
            pltpu.VMEM((MODES * 8, 128), F32),
            pltpu.VMEM((MODES * 8, 128), F32),
            pltpu.VMEM((72, 128), F32),
            pltpu.VMEM((ROWS, 128), F32),
            pltpu.VMEM((3, ROWS, 128), F32),
            pltpu.VMEM((8, 128), F32),
        ],
        cost_estimate=cost(30_000_000, 12_000_000),
        name="backward",
    )(pos, firsts, rim, rate, res, skip, filt, feat, rows, ggr, comb, incoming)


def kernel_e(parts, gfilt, gres, gskip, acc):
    total = parts[0].astype(F32)
    for i in range(1, NCTX):
        total = total + parts[i].astype(F32)
    acc[...] = total
    for k in range(8):
        cols = slice(k * 128, (k + 1) * 128)
        for j in range(3):
            for s in range(TAPS):
                r = (j * 3 + s) * 8 + k
                gfilt[j, s : s + 1, cols] = acc[r : r + 1, :]
        gres[:, cols] = acc[pl.ds(72 + k, MODES, stride=8), :]
        r = (9 + MODES) * 8 + k
        gskip[:, cols] = acc[r : r + 1, :]


def call_e(parts):
    return pl.pallas_call(
        kernel_e,
        out_shape=(
            jax.ShapeDtypeStruct((3, TAPS, CH), F32),
            jax.ShapeDtypeStruct((MODES, CH), F32),
            jax.ShapeDtypeStruct((1, CH), F32),
        ),
        in_specs=[VMEM],
        out_specs=(VMEM,) * 3,
        scratch_shapes=[pltpu.VMEM((SMALL * 8, 128), F32)],
        cost_estimate=cost(1_000_000, 1_000_000),
        name="small_sums",
    )(parts)


def kernel_gg(where, *refs):
    blocks, weight, gg, whole = refs[:NCH], refs[NCH], refs[NCH + 1], refs[NCH + 2]
    step = pl.program_id(0)
    for s in range(NCH):

        @pl.when(step == s)
        def _(s=s):
            block = blocks[s][...]
            part = lax.dot_general(
                block, weight[...], (((1,), (1,)), ((), ())), preferred_element_type=F32
            )
            if s == 0:
                gg[...] = part
            else:
                gg[...] += part
            whole[0] = block[:, :512]
            whole[1] = block[:, 512:]


def call_gg(where, blocks, weight):
    return pl.pallas_call(
        kernel_gg,
        out_shape=(
            jax.ShapeDtypeStruct((TOK, CH), F32),
            jax.ShapeDtypeStruct((NCTX, TOK, 512), BF16),
        ),
        grid_spec=pltpu.PrefetchScalarGridSpec(
            num_scalar_prefetch=1,
            grid=(NCH,),
            in_specs=[pl.BlockSpec((TOK, CH), lambda s, w: (0, 0))] * NCH
            + [pl.BlockSpec((CH, CH), lambda s, w: (0, w[s]))],
            out_specs=(
                pl.BlockSpec((TOK, CH), lambda s, w: (0, 0)),
                pl.BlockSpec((2, TOK, 512), lambda s, w: (w[s], 0, 0)),
            ),
        ),
        cost_estimate=cost(2 * TOK * CH * 8192, 20 << 20),
        name="grad_gated",
    )(where, *blocks, weight)


def kernel_out(where, gated, weight, out):
    out[0] = jnp.dot(gated[...], weight[...], preferred_element_type=F32).astype(out.dtype)


def call_out(where, gated, weight, dtype):
    return pl.pallas_call(
        kernel_out,
        out_shape=jax.ShapeDtypeStruct((4, TOK, CH), dtype),
        grid_spec=pltpu.PrefetchScalarGridSpec(
            num_scalar_prefetch=1,
            grid=(4,),
            in_specs=[
                pl.BlockSpec((TOK, CH), lambda s, w: (0, 0)),
                pl.BlockSpec((CH, CH), lambda s, w: (0, w[s])),
            ],
            out_specs=pl.BlockSpec((1, TOK, CH), lambda s, w: (s, 0, 0)),
        ),
        cost_estimate=cost(TOK * CH * 8192, 10 << 20),
        name="out_part",
    )(where, gated, weight)


X_SIDE = 4


def along_x(a, d):
    route = [(y * 4 + x, y * 4 + (x + d) % 4) for y in range(4) for x in range(4)]
    return lax.ppermute(a, "ctx", route)


def along_y(a, d):
    route = [(y * 4 + x, ((y + d) % 4) * 4 + x) for y in range(4) for x in range(4)]
    return lax.ppermute(a, "ctx", route)


def along_z(a, d):
    route = [(z * 2 + c, ((z + d) % 4) * 2 + c) for z in range(4) for c in range(2)]
    return lax.ppermute(a, "ch", route)


def sibling(a):
    return lax.ppermute(a, "ch", [(i, i ^ 1) for i in range(NCH)])


def next_ctx(a, d):
    route = [(i, i + d) for i in range(NCTX) if 0 <= i + d < NCTX]
    return lax.ppermute(a, "ctx", route)


def to_all_ctx(a):
    return lax.all_to_all(jnp.broadcast_to(a[None], (NCTX,) + a.shape), "ctx", 0, 0, tiled=False)


def on_device(projected, short_filter, decay_rate, residue, skip, state_in, out_weight, cotangent):
    ctx = lax.axis_index("ctx").astype(jnp.int32)
    ch = lax.axis_index("ch").astype(jnp.int32)
    z, core = ch // 2, ch % 2
    pos = ctx[None]
    streams = jnp.transpose(projected, (1, 0, 2))
    skip_row = skip[None]

    hops = (1, 3, 2)
    other = sibling(cotangent)
    remote = [along_z(cotangent, d) for d in hops]
    across = [sibling(a) for a in remote]
    blocks = [cotangent, other] + remote + across
    far = [((z - d) % 4) * 2 for d in hops]
    where = jnp.stack(
        [ch, ch ^ 1] + [f + core for f in far] + [f + 1 - core for f in far]
    ).astype(jnp.int32)

    halo = next_ctx(streams[:, TOK - 2 :, :], 1)
    feat, rows, totals = call_a(streams, halo, short_filter, decay_rate)
    gathered_totals = to_all_ctx(totals)
    gated, comb, incoming = call_b(
        pos, gathered_totals, state_in, decay_rate, residue, skip_row, feat
    )

    gg, whole = call_gg(where, blocks, out_weight)
    ggr, first, rim = call_c(gg, decay_rate, feat, comb, rows)
    firsts = to_all_ctx(first)
    rim_next = next_ctx(rim, -1)

    dest = [((z + d) % 4) * 2 for d in hops] + [z * 2]
    theirs = call_out(jnp.stack([k + 1 - core for k in dest]), gated, out_weight, BF16)
    mine = call_out(jnp.stack([k + core for k in dest]), gated, out_weight, F32)
    pair = mine + sibling(theirs).astype(F32)
    sent = pair[:3].astype(BF16)
    mixed = pair[3]
    for n, d in enumerate(hops):
        mixed = mixed + along_z(sent[n], d).astype(F32)
    mixed_out = mixed.astype(BF16)

    gproj, small, grad_state = call_d(
        pos, firsts, rim_next, decay_rate, residue, skip_row, short_filter,
        feat, rows, ggr, comb, incoming,
    )
    grad_filter, grad_residue, grad_skip = call_e(to_all_ctx(small))

    cot_cols = lax.all_to_all(whole, "ctx", 0, 0, tiled=False).reshape(NCTX * TOK, 512)
    gated_all = to_all_ctx(gated).reshape(NCTX * TOK, CH)
    grad_weight = lax.dot_general(
        cot_cols, gated_all, (((0,), (0,)), ((), ())), preferred_element_type=F32
    ).astype(BF16)

    return (
        mixed_out,
        jnp.transpose(gproj, (1, 0, 2)),
        grad_weight,
        grad_filter,
        grad_residue,
        grad_skip.reshape(CH),
        grad_state,
    )


def solution(mesh):
    in_specs = (
        P("ctx", None, "ch"),
        P(None, None, "ch"),
        P(None, "ch"),
        P(None, "ch"),
        P("ch"),
        P(None, "ch"),
        P("ch", None),
        P("ctx", "ch"),
    )
    out_specs = (
        P("ctx", "ch"),
        P("ctx", None, "ch"),
        P("ctx", "ch"),
        P(None, None, "ch"),
        P(None, "ch"),
        P("ch"),
        P(None, "ch"),
    )
    return jax.shard_map(
        on_device, mesh=mesh, in_specs=in_specs, out_specs=out_specs, check_vma=False
    )
```
